128 devices in a mesh: row: 8 (over z, core), col: 16 (over y, x).
Axes of the slice: x: 4, y: 4, z: 4, core: 2. Of those that a mesh axis runs over, the one named last changes fastest.
Arguments:
- finetune: bfloat16 [8192, 53248], P('row', 'col'), may hold values from -6 to 6
- base_rows: bfloat16 [16384, 53248], P(('row', 'col')), may hold values from -6 to 6
- test_matrix: bfloat16 [256, 53248], P(None, 'col'), may hold values from -0.02734375 to 0.02734375
- base_lengths: int32 [128], replicated, may hold values from 0 to 128, as said below
Outputs:
- basis_out: float32 [8192, 256], P(('row', 'col'))
- coefficients: float32 [256, 53248], P('row', 'col')
The draws below stay inside these ranges and needn't reach their ends.
Inputs may be any that keep to these rules, and one draw needn't show every extreme that they name: Number devices d = row index * 16 + col index. Devices 2m and 2m+1 hold together slab rows m * 128 to m * 128 + 127: device 2m the first base_lengths[2m] of them, device 2m+1 the rest, each from its slot 0 on, so entries 2m and 2m+1 sum to 128. In every draw some device holds 128 rows and some none. Slots past a device's count hold no slab data.
All inputs are finite; a program needn't handle non-finite values.
Results may differ from the reference program's by a relative error of at most 0.014.
Values may be sent and summed in bfloat16 or wider, within the bound.
No kernel may reach another device: no remote copies, remote signals or barrier semaphores. Data moves between devices by JAX's collectives and lax.ppermute only.
A program may use at most 128 MiB of HBM per device.

```python
import math
import jax
import jax.numpy as jnp
from jax import lax

C = 53248
K = 256
SHARDS = 128
CAP = 128
ROWS = 8192


def draw_base_lengths(key, part):
    pair_count = SHARDS // 2
    key_first, key_full, key_empty = jax.random.split(jax.random.fold_in(key, 7), 3)
    first_counts = jax.random.randint(key_first, (pair_count,), 0, CAP + 1)
    full_pair = jax.random.randint(key_full, (), 0, pair_count)
    empty_pair = (full_pair + 1 + jax.random.randint(key_empty, (), 0, pair_count - 1)) % pair_count
    pair_ids = jnp.arange(pair_count)
    first_counts = jnp.where(pair_ids == full_pair, CAP, first_counts)
    first_counts = jnp.where(pair_ids == empty_pair, 0, first_counts)
    return jnp.stack([first_counts, CAP - first_counts], axis=1).reshape(SHARDS).astype(jnp.int32)


def block_scale(own_key, extent, shards, low, largest):
    gain = 1.0
    for axis_at, blocks in shards:
        draws = jax.random.uniform(jax.random.fold_in(jax.random.fold_in(own_key, 6), axis_at), (blocks,), jnp.float32, low / len(shards), largest / len(shards))
        gain = gain * jnp.repeat(jnp.exp(draws), extent[axis_at] // blocks).reshape((-1,) + (1,) * (len(extent) - 1 - axis_at))
    return gain


def noise(rng, dims, width, limit, cuts=(), kind=jnp.bfloat16):
    result = width * jax.random.normal(rng, dims, jnp.float32)
    if cuts:
        result = result * block_scale(rng, dims, cuts, -0.22, 0.18)
    return jnp.clip(result, -limit, limit).astype(kind)


def setup_inputs(seed: int = 0) -> dict:
    seeds = jax.random.split(jax.random.key(seed), 5)
    return {
        "finetune": noise(seeds[0], (ROWS, C), 1.0, 6.0, ((0, 8), (1, 16))),
        "base_rows": noise(seeds[1], (SHARDS * CAP, C), 1.0, 6.0, ((0, 128),)),
        "test_matrix": noise(seeds[2], (K, C), C ** -0.5, 0.02734375, ((1, 16),)),
        "base_lengths": draw_base_lengths(jax.random.fold_in(seeds[4], 71), 0),
    }


def compose(first_half, second_half, first_count):
    capacity = first_half.shape[0]
    row_ids = jnp.arange(capacity)[:, None]
    padded = jnp.concatenate([jnp.zeros_like(second_half), second_half], axis=0)
    shifted = lax.dynamic_slice_in_dim(padded, (capacity - first_count).astype(jnp.int32), capacity, 0)
    return jnp.where(row_ids < first_count, first_half, shifted)

def orthonormal(sketched):
    gram_matrix = jnp.dot(sketched.T, sketched, precision=lax.Precision.HIGHEST)
    factor = jnp.linalg.cholesky(gram_matrix)
    identity = jnp.eye(gram_matrix.shape[0], dtype=gram_matrix.dtype)
    inverse = lax.linalg.triangular_solve(factor, identity, left_side=True, lower=True)
    return jnp.dot(sketched, inverse.T, precision=lax.Precision.HIGHEST)

def reference(finetune, base_rows, test_matrix, base_lengths):
    pair_count = SHARDS // 2
    fine_pairs = finetune.reshape(pair_count, CAP, C)
    base_pairs = base_rows.reshape(pair_count, 2, CAP, C)
    firsts = base_lengths.reshape(pair_count, 2)[:, 0]
    pair_ids = jnp.arange(pair_count).astype(jnp.int32)

    def delta_block(pair_index):
        merged = compose(base_pairs[pair_index, 0], base_pairs[pair_index, 1], firsts[pair_index])
        return fine_pairs[pair_index].astype(jnp.float32) - merged.astype(jnp.float32)

    def sketch(right_side):
        right_wide = right_side.astype(jnp.float32)
        blocks = lax.map(lambda pair_index: jnp.dot(delta_block(pair_index), right_wide.T, precision=lax.Precision.HIGHEST), pair_ids)
        return blocks.reshape(ROWS, K)

    def project(narrow_basis):
        wide_basis = narrow_basis.astype(jnp.float32).reshape(pair_count, CAP, K)

        def advance(running, pair_index):
            return (running + jnp.dot(wide_basis[pair_index].T, delta_block(pair_index), precision=lax.Precision.HIGHEST), None)
        running, unused = lax.scan(advance, jnp.zeros((K, C), jnp.float32), pair_ids)
        return running
    first_basis = orthonormal(sketch(test_matrix))
    projection = project(first_basis.astype(jnp.bfloat16)).astype(jnp.bfloat16)
    second_basis = orthonormal(sketch(projection))
    basis_out = second_basis * math.sqrt(ROWS)
    coefficients = project(second_basis.astype(jnp.bfloat16))
    return (basis_out, coefficients)
```

```python
import functools
import math

import jax
import jax.numpy as jnp
from jax import lax
from jax.experimental import pallas as pl
from jax.experimental.pallas import tpu as pltpu
from jax.sharding import PartitionSpec as P

HIGHEST = lax.Precision.HIGHEST


def swap(value, axis, mask):
    pairs = [(source, source ^ mask) for source in range(lax.axis_size(axis))]
    return lax.ppermute(value, axis, pairs)


def rows_of(tile, index):
    return jnp.broadcast_to(tile[index : index + 1, :], (8, 128))


def column_of(tile, index):
    return jnp.broadcast_to(tile[:, index : index + 1], (8, 128))


def reciprocal_root(value):
    guess = lax.rsqrt(value)
    return guess * (1.5 - 0.5 * value * guess * guess)


def eliminate(tiles):
    count = len(tiles)
    tiles = list(tiles)
    sublane = lax.broadcasted_iota(jnp.int32, (8, 128), 0)
    for at in range(count):
        base = 8 * at
        own = tiles[at]
        columns = [column_of(own, base + j) for j in range(8)]
        cell = {(i, j): rows_of(columns[j], i) for j in range(8) for i in range(j, 8)}
        below = {v: [column_of(tiles[v], base + j) for j in range(8)] for v in range(at + 1, count)}
        lines = [rows_of(own, i) for i in range(8)]
        for j in range(8):
            root = reciprocal_root(cell[j, j])
            lines[j] = lines[j] * root
            low = {i: cell[i, j] * root for i in range(j + 1, 8)}
            for i in range(j + 1, 8):
                for k in range(j + 1, i + 1):
                    cell[i, k] = cell[i, k] - low[i] * low[k]
                lines[i] = lines[i] - low[i] * lines[j]
            for v in below:
                left = below[v][j] * root
                tiles[v] = tiles[v] - left * lines[j]
                for k in range(j + 1, 8):
                    below[v][k] = below[v][k] - left * low[k]
        done = lines[0]
        for j in range(1, 8):
            done = jnp.where(sublane == j, lines[j], done)
        tiles[at] = done
    return tiles


def mul(a, b, dims):
    return lax.dot_general(a, b, (dims, ((), ())), precision=HIGHEST, preferred_element_type=jnp.float32)


def factor_kernel(gram_ref, out_ref, a_ref, x_ref):
    size = gram_ref.shape[0]
    block = 64
    steps = size // block
    a_ref[...] = gram_ref[...]
    row_ids = lax.broadcasted_iota(jnp.int32, (size, size), 0)
    col_ids = lax.broadcasted_iota(jnp.int32, (size, size), 1)
    x_ref[...] = jnp.where(row_ids == col_ids, 1.0, 0.0).astype(jnp.float32)
    small_rows = lax.broadcasted_iota(jnp.int32, (block, block), 0)
    small_cols = lax.broadcasted_iota(jnp.int32, (block, block), 1)
    eye = jnp.where(small_rows == small_cols, 1.0, 0.0).astype(jnp.float32)
    for step in range(steps):
        low, high = step * block, (step + 1) * block
        joined = jnp.concatenate([a_ref[low:high, low:high], eye], axis=1)
        tiles = eliminate([joined[8 * v : 8 * v + 8, :] for v in range(block // 8)])
        inverse = jnp.concatenate(tiles, axis=0)[:, block:]
        inverse = jnp.where(small_rows >= small_cols, inverse, 0.0)
        solved = mul(inverse, x_ref[low:high, :], ((1,), (0,)))
        out_ref[low:high, :] = solved
        if step + 1 < steps:
            left = mul(a_ref[high:, low:high], inverse, ((1,), (1,)))
            x_ref[high:, :] = x_ref[high:, :] - mul(left, solved, ((1,), (0,)))
            a_ref[high:, high:] = a_ref[high:, high:] - mul(left, left, ((1,), (1,)))


def inverse_factor(gram):
    size = gram.shape[0]
    return pl.pallas_call(
        factor_kernel,
        out_shape=jax.ShapeDtypeStruct((size, size), jnp.float32),
        in_specs=[pl.BlockSpec(memory_space=pltpu.VMEM)],
        out_specs=pl.BlockSpec(memory_space=pltpu.VMEM),
        scratch_shapes=[pltpu.VMEM((size, size), jnp.float32)] * 2,
        name="inverse_factor",
    )(gram)


def base_deltas(finetune, base_rows, base_lengths, right_side):
    width = finetune.shape[1]
    slots = base_rows.shape[0]
    col_index = lax.axis_index("col")
    row_index = lax.axis_index("row")
    x, y = col_index % 4, col_index // 4
    parity = x % 2
    pair = x // 2
    device = row_index * lax.axis_size("col") + col_index
    first_count = lax.dynamic_slice_in_dim(base_lengths, device - parity, 1, 0)[0]
    row_ids = lax.broadcasted_iota(jnp.int32, (slots, slots), 0)
    slot_ids = lax.broadcasted_iota(jnp.int32, (slots, slots), 1)
    from_first = (row_ids < first_count) & (slot_ids == row_ids)
    from_second = (row_ids >= first_count) & (slot_ids == row_ids - first_count)
    own_pick = jnp.where(parity == 0, from_first, from_second).astype(jnp.bfloat16)
    partner_pick = jnp.where(parity == 0, from_second, from_first).astype(jnp.bfloat16)

    def block_of(to_y, to_x):
        return lax.dynamic_slice_in_dim(base_rows, (to_y * 4 + to_x) * width, width, 1)

    def merged(own, received):
        total = jnp.dot(own_pick, own, preferred_element_type=jnp.float32)
        total = total + jnp.dot(partner_pick, received, preferred_element_type=jnp.float32)
        return total.astype(jnp.bfloat16)

    order = (2, 1, 3, 0)
    received = {}
    for k in order:
        received[k, "far"] = swap(block_of(y ^ k, x ^ 2), "col", 1)
        received[k, "near"] = swap(block_of(y ^ k, x ^ 1), "col", 1)
    arrived = []
    for k in order:
        far = merged(block_of(y ^ k, x ^ 3), received[k, "far"])
        other = swap(far, "col", 3)
        near = merged(block_of(y ^ k, x), received[k, "near"])
        if k:
            near = swap(near, "col", 4 * k)
            other = swap(other, "col", 4 * k)
        arrived.append(((y ^ k) * 2 + pair, near))
        arrived.append(((y ^ k) * 2 + 1 - pair, other))
    fine_blocks = finetune.reshape(-1, slots, width)
    deltas = jnp.zeros(fine_blocks.shape, jnp.bfloat16)
    sketch = jnp.zeros((fine_blocks.shape[0], slots, right_side.shape[0]), jnp.float32)
    for index, piece in arrived:
        fine = lax.dynamic_index_in_dim(fine_blocks, index, 0, keepdims=False)
        delta = (fine.astype(jnp.float32) - piece.astype(jnp.float32)).astype(jnp.bfloat16)
        deltas = lax.dynamic_update_index_in_dim(deltas, delta, index, 0)
        part = against(delta, right_side)
        sketch = lax.dynamic_update_index_in_dim(sketch, part, index, 0)
    return deltas.reshape(finetune.shape), sketch.reshape(-1, right_side.shape[0])


def against(left_side, right_side):
    return lax.dot_general(
        left_side, right_side, (((1,), (1,)), ((), ())), preferred_element_type=jnp.float32
    )


def contract_rows(left_side, right_side):
    return lax.dot_general(
        left_side, right_side, (((0,), (0,)), ((), ())), preferred_element_type=jnp.float32
    )


def own_sketch_rows(partial_value):
    count = lax.axis_size("col")
    pieces = partial_value.reshape(count, -1, partial_value.shape[1])
    pieces = lax.all_to_all(pieces, "col", split_axis=0, concat_axis=0, tiled=True)
    return pieces.sum(0)


def group_sketch(own_rows):
    count = lax.axis_size("col")
    copies = jnp.broadcast_to(own_rows[None], (count,) + own_rows.shape)
    copies = lax.all_to_all(copies, "col", split_axis=0, concat_axis=0, tiled=True)
    return copies.reshape(-1, own_rows.shape[1])


def total_gram(gram):
    core = lax.axis_index("row") % 2
    half = gram.shape[0] // 2
    halves = gram.reshape(2, half, -1)
    keep = lax.dynamic_index_in_dim(halves, core, 0, keepdims=False)
    give = lax.dynamic_index_in_dim(halves, 1 - core, 0, keepdims=False)
    mine = keep + swap(give, "row", 1)
    near, far, back = swap(mine, "row", 2), swap(mine, "row", 4), swap(mine, "row", 6)
    z = lax.axis_index("row") // 2
    low = mine + near
    high = far + back
    mine = low + high
    other = swap(mine, "row", 1)
    return jnp.concatenate(
        [jnp.where(core == 0, mine, other), jnp.where(core == 0, other, mine)], axis=0
    )


def scattered_projection(narrow, deltas):
    row_index = lax.axis_index("row")
    core, z = row_index % 2, row_index // 2
    rank = narrow.shape[1]
    share = rank // 8
    blocks = narrow.reshape(narrow.shape[0], 4, 2, share)

    def half(which):
        side = lax.dynamic_index_in_dim(blocks, which, 2, keepdims=False)
        return contract_rows(side.reshape(narrow.shape[0], rank // 2), deltas)

    give = half(1 - core).astype(jnp.bfloat16)
    received = swap(give, "row", 1)
    keep = half(core) + received.astype(jnp.float32)
    quarters = keep.reshape(4, share, -1)

    def quarter(which):
        return lax.dynamic_index_in_dim(quarters, which, 0, keepdims=False)

    incoming = [swap(quarter(z ^ j).astype(jnp.bfloat16), "row", 2 * j) for j in (2, 1, 3)]
    total = quarter(z)
    for piece in incoming:
        total = total + piece.astype(jnp.float32)
    return total


def gathered_halves(share):
    row_index = lax.axis_index("row")
    z = row_index // 2
    pieces = [share] + [swap(share, "row", 2 * j) for j in (1, 2, 3)]
    order = jnp.stack(pieces)
    own = jnp.stack([lax.dynamic_index_in_dim(order, z ^ j, 0, keepdims=False) for j in range(4)])
    own = own.reshape(-1, share.shape[1])
    return own, swap(own, "row", 1)


def basis_of(partial_value, scale):
    own_rows = own_sketch_rows(partial_value)
    group_rows = group_sketch(own_rows)
    gram = total_gram(mul(group_rows, group_rows, ((0,), (0,))))
    inverse = inverse_factor(gram)
    narrow = mul(group_rows, inverse, ((1,), (1,))).astype(jnp.bfloat16)
    if scale is None:
        return narrow, None
    return narrow, mul(own_rows, inverse, ((1,), (1,))) * scale


def per_device(finetune, base_rows, test_matrix, base_lengths):
    total_rows = base_rows.shape[0] // 2 * lax.axis_size("row") * lax.axis_size("col")
    core = lax.axis_index("row") % 2
    deltas, partial_value = base_deltas(finetune, base_rows, base_lengths, test_matrix)
    narrow, _ = basis_of(partial_value, None)
    share = scattered_projection(narrow, deltas).astype(jnp.bfloat16)
    own, other = gathered_halves(share)
    own_side = against(deltas, own).reshape(-1, 4, share.shape[0])
    other_side = against(deltas, other).reshape(-1, 4, share.shape[0])
    even = jnp.where(core == 0, own_side, other_side)
    odd = jnp.where(core == 0, other_side, own_side)
    partial_value = jnp.stack([even, odd], axis=2).reshape(deltas.shape[0], -1)
    narrow, basis_out = basis_of(partial_value, math.sqrt(total_rows))
    coefficients = scattered_projection(narrow, deltas)
    return basis_out, coefficients


def solution(mesh):
    return jax.shard_map(
        per_device,
        mesh=mesh,
        in_specs=(P("row", "col"), P(("row", "col"), None), P(None, "col"), P()),
        out_specs=(P(("row", "col"), None), P("row", "col")),
        check_vma=False,
    )
```
